256 devices in a mesh: blk: 32 (over x_hi, z, core), fsdp: 8 (over y, x_lo).
Axes of the slice: x: 4 (x_hi: 2, x_lo: 2; x = x_hi * 2 + x_lo), y: 4, z: 8, core: 2. Of those that a mesh axis runs over, the one named last changes fastest.
Arguments:
- params: float32 [32, 4096, 1024], P('blk', 'fsdp'), may hold values from -6 to 6
- inputs: bfloat16 [32, 7168, 4096], P('blk', 'fsdp'), may hold values from -6 to 6
- cotangent: bfloat16 [32, 7168, 1024], P('blk', 'fsdp'), may hold values from -6 to 6
- mix: int32 [32, 3], replicated, may hold values from 8 to 48, as said below
Outputs:
- new_params: float32 [32, 4096, 1024], P('blk', 'fsdp')
The draws below stay inside these ranges and needn't reach their ends.
Inputs may be any that keep to these rules, and one draw needn't show every extreme that they name: `mix`: each row holds three positive numerators that sum to 64.
All inputs are finite; a program needn't handle non-finite values.
Results may differ from the reference program's by a relative error of at most 0.0003.
Values may be sent and summed in bfloat16 or wider, within the bound.
A program may use at most 128 MiB of HBM per device.

```python
import jax
import jax.numpy as jnp
from jax import lax

D = 4096
KV = 1024
TOK_DEV = 896
MIX_DENOM = 64
TOKENS = 7168
NREP = 32
N_FSDP = 8


def draw_mix(key, part):
    key_left, key_right = jax.random.split(jax.random.fold_in(key, 17))
    left_part = jax.random.randint(key_left, (NREP, 1), 8, 25)
    right_part = jax.random.randint(key_right, (NREP, 1), 8, 25)
    return jnp.concatenate([left_part, MIX_DENOM - left_part - right_part, right_part], axis=1).astype(jnp.int32)


def block_levels(rng, extent, cuts, least, top_value):
    def one(dim, blocks):
        draws = jax.random.uniform(jax.random.fold_in(jax.random.fold_in(rng, 6), dim), (blocks,), jnp.float32, least / len(cuts), top_value / len(cuts))
        return jnp.repeat(jnp.exp(draws), extent[dim] // blocks).reshape((-1,) + (1,) * (len(extent) - dim - 1))

    gain = one(*cuts[0])
    for cut in cuts[1:]:
        gain = gain * one(*cut)
    return gain


def scatter_about(key, dims, scale, most, pieces=(), kind=jnp.bfloat16):
    drawn = jax.random.normal(key, dims, jnp.float32) * scale
    if len(pieces) > 0:
        drawn = block_levels(key, dims, pieces, -0.22, 0.18) * drawn
    return jnp.clip(drawn, min=-most, max=most).astype(kind)


def setup_inputs(seed: int = 0) -> dict:
    keys = jax.random.split(jax.random.key(seed), 5)
    params = scatter_about(keys[0], (NREP, D, KV), 1.0, 6.0, ((0, 32), (1, 8)), jnp.float32)
    inputs = scatter_about(keys[1], (NREP, TOKENS, D), 1.0, 6.0, ((0, 32), (1, 8)))
    cotangent = scatter_about(keys[2], (NREP, TOKENS, KV), 1.0, 6.0, ((0, 32), (1, 8)))
    mix = draw_mix(jax.random.fold_in(keys[4], 71), 0)
    return dict(params=params, inputs=inputs, cotangent=cotangent, mix=mix)


RATE = 0.03

def replica_grad(pair):
    inputs_r, cot_r = pair
    x_blocks = inputs_r.reshape(N_FSDP, TOK_DEV, D)
    c_blocks = cot_r.reshape(N_FSDP, TOK_DEV, KV)

    def add_block(total, blocks):
        x_block, c_block = blocks
        part = jnp.dot(x_block.T, c_block, preferred_element_type=jnp.float32)
        return (total + part, None)
    total, unused = lax.scan(add_block, jnp.zeros((D, KV), jnp.float32), (x_blocks, c_blocks))
    return total

def reference(params, inputs, cotangent, mix):
    gradient = lax.map(replica_grad, (inputs, cotangent))
    coeff = mix.astype(jnp.float32) / MIX_DENOM
    c_left = coeff[:, 0][:, None, None]
    c_self = coeff[:, 1][:, None, None]
    c_right = coeff[:, 2][:, None, None]
    mixed_params = c_left * jnp.roll(params, 1, 0) + c_self * params + c_right * jnp.roll(params, -1, 0)
    mixed_grads = c_left * jnp.roll(gradient, 1, 0) + c_self * gradient + c_right * jnp.roll(gradient, -1, 0)
    return mixed_params - RATE * mixed_grads
```

```python
import functools

import jax
import jax.numpy as jnp
from jax import lax
from jax.experimental import pallas as pl
from jax.experimental.pallas import tpu as pltpu
from jax.sharding import PartitionSpec as P

MIX_DENOM = 64
RATE = 0.03
LEVELS = 32767.0
TINY = 1e-30
MESH = pl.DeviceIdType.MESH

NY = 4
NX = 2
NSH = NY * NX
TILE = 128
R = 64
LA = 384

UP, DN = 0, 1


def message_shapes(kv):
    h, lb = R // 2, kv - LA
    return dict(
        ax=(1, NY, R, LA),
        by1=(2, 4, h, lb),
        by2=(2, 2, h, lb),
        bx=(1, 2, h, lb),
        ay1=(2, 2, h, LA),
        ay2=(2, 1, h, LA),
        u=(1, R // 16, 16, kv),
    )


def kernel(shapes, nrep, k_chunks, *refs):
    names = list(shapes)
    (params, inputs, cot_hbm, mix, out), refs = refs[:5], refs[5:]
    nm = len(names)
    sendq, sends = dict(zip(names, refs[:nm])), dict(zip(names, refs[nm : 2 * nm]))
    recvq, recvs = dict(zip(names, refs[2 * nm : 3 * nm])), dict(zip(names, refs[3 * nm : 4 * nm]))
    refs = refs[4 * nm :]
    sem_s, sem_r = dict(zip(names, refs[:nm])), dict(zip(names, refs[nm : 2 * nm]))
    part, xbuf, cot, pbuf, obuf, sem_x, sem_c, sem_p, sem_o = refs[2 * nm :]

    tokens, kv = cot.shape
    n_tiles = xbuf.shape[0]
    sub = TILE // R
    shard_rows = TILE * n_tiles
    h = R // 2
    lb = kv - LA
    A, B = slice(0, LA), slice(LA, kv)
    H = (slice(0, h), slice(h, R))

    rep = lax.axis_index("blk")
    fs = lax.axis_index("fsdp")
    y, x = fs // NX, fs % NX
    y_up, y_dn, y_far = (y + 1) % NY, (y + NY - 1) % NY, (y + 2) % NY
    dev = dict(
        up=(rep, y_up * NX + x),
        dn=(rep, y_dn * NX + x),
        x=(rep, y * NX + (1 - x)),
        right=((rep + 1) % nrep, fs),
        left=((rep + nrep - 1) % nrep, fs),
    )

    def shard(yy, xx):
        return yy * NX + xx

    def load_x(c, f):
        return pltpu.make_async_copy(
            inputs.at[0, :, pl.ds(f * shard_rows + c * TILE, TILE)],
            xbuf.at[c, :, pl.ds(f * TILE, TILE)],
            sem_x.at[c, f],
        )

    load_cot = pltpu.make_async_copy(cot_hbm.at[0], cot, sem_c)
    load_p = pltpu.make_async_copy(params.at[0], pbuf, sem_p)
    load_cot.start()
    for c in range(n_tiles):
        for f in range(NSH):
            load_x(c, f).start()
    load_p.start()

    barrier = pltpu.get_barrier_semaphore()
    for d in dev.values():
        pl.semaphore_signal(barrier, inc=1, device_id=d, device_id_type=MESH)
    pl.semaphore_wait(barrier, len(dev))

    def copies(name, d, k, to):
        return [
            pltpu.make_async_remote_copy(
                src_ref=src.at[0 if name == "u" else d, k],
                dst_ref=dst.at[d, k],
                send_sem=sem_s[name].at[d, i, k],
                recv_sem=sem_r[name].at[d, i, k],
                device_id=dev[to],
                device_id_type=MESH,
            )
            for i, (src, dst) in enumerate(
                ((sendq[name], recvq[name]), (sends[name], recvs[name]))
            )
        ]

    TO = dict(ax=("x",), bx=("x",), u=("right", "left"))

    def target(name, d):
        return TO.get(name, ("up", "dn"))[d]

    def send(name, d, k):
        for c in copies(name, d, k, target(name, d)):
            c.start()

    def arrived(name, d, k):
        for c in copies(name, d, k, target(name, d)):
            c.wait_recv()

    def sent(name, d, k):
        for c in copies(name, d, k, target(name, d)):
            c.wait_send()

    def encode(name, d, k, blocks):
        top = functools.reduce(jnp.maximum, [jnp.abs(b()) for b in blocks])
        top = jnp.maximum(jnp.max(top, axis=0, keepdims=True), TINY)
        sends[name][d, k] = top * (1.0 / LEVELS)
        inv = LEVELS / top
        for i, b in enumerate(blocks):
            sendq[name][d, k, i] = jnp.round(b() * inv).astype(jnp.int32).astype(jnp.int16)

    def decode(name, d, k, i, rows=None):
        q = recvq[name][d, k, i] if rows is None else recvq[name][d, k, i, rows]
        return q.astype(jnp.int32).astype(jnp.float32) * recvs[name][d, k]

    def at(k, f, rows, cols):
        return lambda: part[k, f, rows, cols]

    def multiply(c, j):
        lhs = xbuf[c, :, pl.ds(pl.multiple_of(j * (2 * TILE), 2 * TILE), 2 * TILE)]
        prod = lax.dot_general(
            lhs, cot[...], (((0,), (0,)), ((), ())), preferred_element_type=jnp.float32
        )
        for a in range(2):
            for i in range(sub):
                lo = a * TILE + i * R
                part[c * sub + i, 2 * j + a] = prod[lo : lo + R]

    def wait_x(c):
        for f in range(NSH):
            load_x(c, f).wait()

    def stage1(k):
        encode("ax", 0, k, [at(k, shard(yy, 1 - x), slice(0, R), A) for yy in range(NY)])
        send("ax", 0, k)
        for d, near, relay, plain in ((UP, y_up, H[1], H[0]), (DN, y_dn, H[0], H[1])):
            encode(
                "by1",
                d,
                k,
                [at(k, shard(y_far, xx), relay, B) for xx in range(NX)]
                + [at(k, shard(near, xx), plain, B) for xx in range(NX)],
            )
            send("by1", d, k)

    def stage2(k):
        for d, near, relay in ((UP, y_up, H[1]), (DN, y_dn, H[0])):
            arrived("by1", d, k)
            for xx in range(NX):
                part[k, shard(near, xx), relay, B] += decode("by1", d, k, xx)
            encode("by2", d, k, [at(k, shard(near, xx), relay, B) for xx in range(NX)])
            send("by2", d, k)
        arrived("ax", 0, k)
        for yy in range(NY):
            part[k, shard(yy, x), :, A] += decode("ax", 0, k, yy)
        for d, near, relay, plain in ((UP, y_up, H[1], H[0]), (DN, y_dn, H[0], H[1])):
            encode("ay1", d, k, [at(k, shard(y_far, x), relay, A), at(k, shard(near, x), plain, A)])
            send("ay1", d, k)

    def stage3(k):
        for d in (UP, DN):
            arrived("by2", d, k)
        for xx in (1 - x, x):
            part[k, shard(y, xx), H[0], B] += decode("by1", UP, k, 2 + xx) + decode("by2", DN, k, xx)
            part[k, shard(y, xx), H[1], B] += decode("by1", DN, k, 2 + xx) + decode("by2", UP, k, xx)
        encode("bx", 0, k, [at(k, shard(y, 1 - x), rows, B) for rows in H])
        send("bx", 0, k)
        for d, near, relay in ((UP, y_up, H[1]), (DN, y_dn, H[0])):
            arrived("ay1", d, k)
            part[k, shard(near, x), relay, A] += decode("ay1", d, k, 0)
            encode("ay2", d, k, [at(k, shard(near, x), relay, A)])
            send("ay2", d, k)

    def stage4(k):
        for d in (UP, DN):
            arrived("ay2", d, k)
        arrived("bx", 0, k)
        mine = shard(y, x)
        base = pl.multiple_of(k * R, R)
        for half in (0, 1):
            d1, d2 = ((UP, DN), (DN, UP))[half]
            rows = H[half]
            prow = pl.ds(base + half * h, h)
            g = part[k, mine, rows, A] + decode("ay1", d1, k, 1) + decode("ay2", d2, k, 0)
            part[k, mine, rows, A] = pbuf[prow, A] - RATE * g
            g = part[k, mine, rows, B] + decode("bx", 0, k, half)
            part[k, mine, rows, B] = pbuf[prow, B] - RATE * g
        n = R // 16
        encode("u", 0, k, [at(k, mine, slice(16 * i, 16 * i + 16), slice(0, kv)) for i in range(n)])
        for d in (0, 1):
            send("u", d, k)

    c_left = mix[rep, 0].astype(jnp.float32) * (1.0 / MIX_DENOM)
    c_self = mix[rep, 1].astype(jnp.float32) * (1.0 / MIX_DENOM)
    c_right = mix[rep, 2].astype(jnp.float32) * (1.0 / MIX_DENOM)

    def store(k):
        base = pl.multiple_of(k * R, R)
        return pltpu.make_async_copy(obuf.at[k], out.at[0, pl.ds(base, R)], sem_o.at[k])

    def stage5(k):
        for d in (0, 1):
            arrived("u", d, k)
        mine = shard(y, x)
        for i in range(R // 16):
            rows = slice(16 * i, 16 * i + 16)
            obuf[k, rows] = (
                c_left * decode("u", 0, k, i)
                + c_self * part[k, mine, rows]
                + c_right * decode("u", 1, k, i)
            )
        store(k).start()

    load_cot.wait()
    wait_x(0)
    per_tile = NSH // 2

    @pl.loop(0, per_tile)
    def _(j):
        multiply(0, j)

    share = per_tile // sub

    @pl.loop(0, k_chunks + 4)
    def _(s):
        @pl.when(s < k_chunks)
        def _():
            stage1(s)

        c = s // sub + 1

        @pl.when(c < n_tiles)
        def _():
            @pl.when(s % sub == 0)
            def _():
                for f in range(NSH):
                    load_x(c, f).wait()

            @pl.loop(0, share)
            def _(j):
                multiply(c, (s % sub) * share + j)

        @pl.when(s == 0)
        def _():
            load_p.wait()

        for lag, stage in ((1, stage2), (2, stage3), (3, stage4), (4, stage5)):

            @pl.when((s >= lag) & (s < k_chunks + lag))
            def _(lag=lag, stage=stage):
                stage(s - lag)

    @pl.loop(0, k_chunks)
    def _(k):
        for name, shape in shapes.items():
            for d in range(2 if name == "u" else shape[0]):
                sent(name, d, k)
        store(k).wait()


def on_device(nrep, params, inputs, cotangent, mix):
    _, tokens, width = inputs.shape
    kv = cotangent.shape[-1]
    rows = params.shape[1]
    n_tiles = rows // TILE
    k_chunks = rows // R
    shapes = message_shapes(kv)
    names = list(shapes)
    landing = {n: (2 if n == "u" else s[0],) + s[1:] for n, s in shapes.items()}

    def data(table):
        return [pltpu.VMEM((s[0], k_chunks) + s[1:], jnp.int16) for s in table.values()]

    def scales(table):
        return [pltpu.VMEM((s[0], k_chunks, 1, s[3]), jnp.float32) for s in table.values()]

    sems = [pltpu.SemaphoreType.DMA((landing[n][0], 2, k_chunks)) for n in names]
    scratch = (
        data(shapes)
        + scales(shapes)
        + data(landing)
        + scales(landing)
        + sems
        + sems
        + [
            pltpu.VMEM((k_chunks, NSH, R, kv), jnp.float32),
            pltpu.VMEM((n_tiles, tokens, NSH * TILE), jnp.bfloat16),
            pltpu.VMEM((tokens, kv), jnp.bfloat16),
            pltpu.VMEM((rows, kv), jnp.float32),
            pltpu.VMEM((k_chunks, R, kv), jnp.float32),
            pltpu.SemaphoreType.DMA((n_tiles, NSH)),
            pltpu.SemaphoreType.DMA,
            pltpu.SemaphoreType.DMA,
            pltpu.SemaphoreType.DMA((k_chunks,)),
        ]
    )
    hbm = pl.BlockSpec(memory_space=pl.ANY)
    return pl.pallas_call(
        functools.partial(kernel, shapes, nrep, k_chunks),
        out_shape=jax.ShapeDtypeStruct(params.shape, jnp.float32),
        in_specs=[hbm, hbm, hbm, pl.BlockSpec(memory_space=pltpu.SMEM)],
        out_specs=hbm,
        scratch_shapes=scratch,
        compiler_params=pltpu.CompilerParams(
            collective_id=0, has_side_effects=True, vmem_limit_bytes=62 << 20
        ),
        name="gossip_step",
    )(params, inputs, cotangent, mix)


def solution(mesh):
    return jax.shard_map(
        functools.partial(on_device, mesh.shape["blk"]),
        mesh=mesh,
        in_specs=(P("blk", "fsdp", None), P("blk", "fsdp", None), P("blk", "fsdp", None), P()),
        out_specs=P("blk", "fsdp", None),
        check_vma=False,
    )
```

```python
import functools

import jax
import jax.numpy as jnp
from jax import lax
from jax.experimental import pallas as pl
from jax.experimental.pallas import tpu as pltpu
from jax.sharding import PartitionSpec as P

MIX_DENOM = 64
RATE = 0.03
LEVELS = 32767.0
TINY = 1e-30
MESH = pl.DeviceIdType.MESH

NY = 4
NX = 2
NSH = NY * NX
TILE = 128
R = 64
LA = 384

UP, DN = 0, 1
CUT = 256


def message_shapes(kv):
    h, lb = R // 2, kv - LA
    return dict(
        ax=(1, NY, R, LA),
        by1=(2, 4, h, lb),
        by2=(2, 2, h, lb),
        bx=(1, 2, h, lb),
        ay1=(2, 2, h, LA),
        ay2=(2, 1, h, LA),
        u=(1, R // 16, 16, kv),
    )


def kernel(shapes, nrep, k_chunks, *refs):
    names = list(shapes)
    (params, inputs, cot_hbm, mix, out), refs = refs[:5], refs[5:]
    nm = len(names)
    sendq, sends = dict(zip(names, refs[:nm])), dict(zip(names, refs[nm : 2 * nm]))
    recvq, recvs = dict(zip(names, refs[2 * nm : 3 * nm])), dict(zip(names, refs[3 * nm : 4 * nm]))
    refs = refs[4 * nm :]
    sem_s, sem_r = dict(zip(names, refs[:nm])), dict(zip(names, refs[nm : 2 * nm]))
    part, xbuf, cot, pbuf, mbuf, sem_x, sem_c, sem_p, sem_m = refs[2 * nm :]

    tokens, kv = cot.shape
    n_tiles = xbuf.shape[0]
    sub = TILE // R
    shard_rows = TILE * n_tiles
    h = R // 2
    lb = kv - LA
    A, B = slice(0, LA), slice(LA, kv)
    H = (slice(0, h), slice(h, R))

    rep = lax.axis_index("blk")
    fs = lax.axis_index("fsdp")
    y, x = fs // NX, fs % NX
    y_up, y_dn, y_far = (y + 1) % NY, (y + NY - 1) % NY, (y + 2) % NY
    dev = dict(
        up=(rep, y_up * NX + x),
        dn=(rep, y_dn * NX + x),
        x=(rep, y * NX + (1 - x)),
        right=((rep + 1) % nrep, fs),
        left=((rep + nrep - 1) % nrep, fs),
    )

    def shard(yy, xx):
        return yy * NX + xx

    def load_x(c, f):
        return pltpu.make_async_copy(
            inputs.at[0, :, pl.ds(pl.multiple_of(f * shard_rows + c * TILE, TILE), TILE)],
            xbuf.at[c, :, pl.ds(pl.multiple_of(f * TILE, TILE), TILE)],
            sem_x.at[c, f],
        )

    early, late = slice(CUT, kv), slice(0, CUT)

    def load_cot(i, cols):
        return pltpu.make_async_copy(cot_hbm.at[0, :, cols], cot.at[:, cols], sem_c.at[i])

    load_p = pltpu.make_async_copy(params.at[0], pbuf, sem_p)
    load_mix = pltpu.make_async_copy(mix, mbuf, sem_m)
    def tile_x(yy):
        return [load_x(0, shard(yy, xx)) for xx in range(NX)]

    load_cot(0, early).start()
    for yy in (y_far, y_up):
        for load in tile_x(yy):
            load.start()
    for yy in (y_dn, y):
        for load in tile_x(yy):
            load.start()
    load_cot(1, late).start()

    barrier = pltpu.get_barrier_semaphore()
    for d in dev.values():
        pl.semaphore_signal(barrier, inc=1, device_id=d, device_id_type=MESH)

    def copies(name, d, k, to):
        return [
            pltpu.make_async_remote_copy(
                src_ref=src.at[0 if name == "u" else d, k],
                dst_ref=dst.at[d, k],
                send_sem=sem_s[name].at[d, i, k],
                recv_sem=sem_r[name].at[d, i, k],
                device_id=dev[to],
                device_id_type=MESH,
            )
            for i, (src, dst) in enumerate(
                ((sendq[name], recvq[name]), (sends[name], recvs[name]))
            )
        ]

    TO = dict(ax=("x",), bx=("x",), u=("right", "left"))

    def target(name, d):
        return TO.get(name, ("up", "dn"))[d]

    def send(name, d, k):
        for c in copies(name, d, k, target(name, d)):
            c.start()

    def arrived(name, d, k):
        for c in copies(name, d, k, target(name, d)):
            c.wait_recv()

    def sent(name, d, k):
        for c in copies(name, d, k, target(name, d)):
            c.wait_send()

    def encode(name, d, k, blocks):
        top = functools.reduce(jnp.maximum, [jnp.abs(b()) for b in blocks])
        top = jnp.maximum(jnp.max(top, axis=0, keepdims=True), TINY)
        sends[name][d, k] = top * (1.0 / LEVELS)
        inv = LEVELS / top
        for i, b in enumerate(blocks):
            sendq[name][d, k, i] = jnp.round(b() * inv).astype(jnp.int32).astype(jnp.int16)

    def decode(name, d, k, i, rows=None):
        q = recvq[name][d, k, i] if rows is None else recvq[name][d, k, i, rows]
        return q.astype(jnp.int32).astype(jnp.float32) * recvs[name][d, k]

    def at(k, f, rows, cols):
        return lambda: part[k, f, rows, cols]

    def multiply(c, j, cols=slice(0, kv)):
        lhs = xbuf[c, :, pl.ds(pl.multiple_of(j * (2 * TILE), 2 * TILE), 2 * TILE)]
        prod = lax.dot_general(
            lhs, cot[:, cols], (((0,), (0,)), ((), ())), preferred_element_type=jnp.float32
        )
        for a in range(2):
            for i in range(sub):
                lo = a * TILE + i * R
                part[c * sub + i, 2 * j + a, :, cols] = prod[lo : lo + R]

    BY1 = {UP: (y_up, H[1], H[0]), DN: (y_dn, H[0], H[1])}

    def first_y(k, d):
        near, relay, plain = BY1[d]
        encode(
            "by1",
            d,
            k,
            [at(k, shard(y_far, xx), relay, B) for xx in range(NX)]
            + [at(k, shard(near, xx), plain, B) for xx in range(NX)],
        )
        send("by1", d, k)

    def first_x(k):
        encode("ax", 0, k, [at(k, shard(yy, 1 - x), slice(0, R), A) for yy in range(NY)])
        send("ax", 0, k)

    def stage1(k):
        first_x(k)
        for d in (UP, DN):
            first_y(k, d)

    def stage2(k):
        for d, near, relay in ((UP, y_up, H[1]), (DN, y_dn, H[0])):
            arrived("by1", d, k)
            for xx in range(NX):
                part[k, shard(near, xx), relay, B] += decode("by1", d, k, xx)
            encode("by2", d, k, [at(k, shard(near, xx), relay, B) for xx in range(NX)])
            send("by2", d, k)
        arrived("ax", 0, k)
        for yy in range(NY):
            part[k, shard(yy, x), :, A] += decode("ax", 0, k, yy)
        for d, near, relay, plain in ((UP, y_up, H[1], H[0]), (DN, y_dn, H[0], H[1])):
            encode("ay1", d, k, [at(k, shard(y_far, x), relay, A), at(k, shard(near, x), plain, A)])
            send("ay1", d, k)

    def stage3(k):
        for d in (UP, DN):
            arrived("by2", d, k)
        for xx in (1 - x, x):
            part[k, shard(y, xx), H[0], B] += decode("by1", UP, k, 2 + xx) + decode("by2", DN, k, xx)
            part[k, shard(y, xx), H[1], B] += decode("by1", DN, k, 2 + xx) + decode("by2", UP, k, xx)
        encode("bx", 0, k, [at(k, shard(y, 1 - x), rows, B) for rows in H])
        send("bx", 0, k)
        for d, near, relay in ((UP, y_up, H[1]), (DN, y_dn, H[0])):
            arrived("ay1", d, k)
            part[k, shard(near, x), relay, A] += decode("ay1", d, k, 0)
            encode("ay2", d, k, [at(k, shard(near, x), relay, A)])
            send("ay2", d, k)

    def stage4(k):
        for d in (UP, DN):
            arrived("ay2", d, k)
        arrived("bx", 0, k)
        mine = shard(y, x)
        base = pl.multiple_of(k * R, R)
        for half in (0, 1):
            d1, d2 = ((UP, DN), (DN, UP))[half]
            rows = H[half]
            prow = pl.ds(base + half * h, h)
            g = part[k, mine, rows, A] + decode("ay1", d1, k, 1) + decode("ay2", d2, k, 0)
            part[k, mine, rows, A] = pbuf[prow, A] - RATE * g
            g = part[k, mine, rows, B] + decode("bx", 0, k, half)
            part[k, mine, rows, B] = pbuf[prow, B] - RATE * g
        n = R // 16
        encode("u", 0, k, [at(k, mine, slice(16 * i, 16 * i + 16), slice(0, kv)) for i in range(n)])
        for d in (0, 1):
            send("u", d, k)

    def stage5(k):
        for d in (0, 1):
            arrived("u", d, k)
        mine = shard(y, x)
        column = lax.broadcasted_iota(jnp.int32, mbuf.shape, 1) == rep
        coeff = jnp.where(column, mbuf[...].astype(jnp.float32) * (1.0 / MIX_DENOM), 0.0)
        coeff = jnp.sum(coeff, axis=1, keepdims=True)
        c_left, c_self, c_right = coeff[0:1], coeff[1:2], coeff[2:3]
        for i in range(R // 16):
            rows = slice(16 * i, 16 * i + 16)
            out[0, pl.ds(pl.multiple_of(k * R + 16 * i, 16), 16)] = (
                c_left * decode("u", 0, k, i)
                + c_self * part[k, mine, rows]
                + c_right * decode("u", 1, k, i)
            )

    load_cot(0, early).wait()
    for yy in (y_far, y_up):
        for load in tile_x(yy):
            load.wait()
        multiply(0, yy, early)
    pl.semaphore_wait(barrier, len(dev))
    first_y(0, UP)
    for yy in (y_dn, y):
        for load in tile_x(yy):
            load.wait()
    load_cot(1, late).wait()
    for c in range(1, n_tiles):
        for f in range(NSH):
            load_x(c, f).start()
    load_p.start()
    load_mix.start()
    multiply(0, y_dn, early)
    first_y(0, DN)

    per_tile = NSH // 2

    @pl.loop(0, per_tile)
    def _(j):
        multiply(0, j, late)

    multiply(0, y, early)
    first_x(0)

    share = per_tile // sub

    @pl.loop(0, k_chunks + 4)
    def _(s):
        @pl.when((s >= 1) & (s < k_chunks))
        def _():
            stage1(s)

        c = s // sub + 1

        @pl.when(c < n_tiles)
        def _():
            @pl.when(s % sub == 0)
            def _():
                for f in range(NSH):
                    load_x(c, f).wait()

            @pl.loop(0, share)
            def _(j):
                multiply(c, (s % sub) * share + j)

        @pl.when(s == 0)
        def _():
            load_p.wait()
            load_mix.wait()

        for lag, stage in ((1, stage2), (2, stage3), (3, stage4), (4, stage5)):

            @pl.when((s >= lag) & (s < k_chunks + lag))
            def _(lag=lag, stage=stage):
                stage(s - lag)

    @pl.loop(0, k_chunks)
    def _(k):
        for name, shape in shapes.items():
            for d in range(2 if name == "u" else shape[0]):
                sent(name, d, k)


def on_device(nrep, params, inputs, cotangent, mix):
    _, tokens, width = inputs.shape
    kv = cotangent.shape[-1]
    rows = params.shape[1]
    n_tiles = rows // TILE
    k_chunks = rows // R
    shapes = message_shapes(kv)
    names = list(shapes)
    landing = {n: (2 if n == "u" else s[0],) + s[1:] for n, s in shapes.items()}

    def data(table):
        return [pltpu.VMEM((s[0], k_chunks) + s[1:], jnp.int16) for s in table.values()]

    def scales(table):
        return [pltpu.VMEM((s[0], k_chunks, 1, s[3]), jnp.float32) for s in table.values()]

    sems = [pltpu.SemaphoreType.DMA((landing[n][0], 2, k_chunks)) for n in names]
    scratch = (
        data(shapes)
        + scales(shapes)
        + data(landing)
        + scales(landing)
        + sems
        + sems
        + [
            pltpu.VMEM((k_chunks, NSH, R, kv), jnp.float32),
            pltpu.VMEM((n_tiles, tokens, NSH * TILE), jnp.bfloat16),
            pltpu.VMEM((tokens, kv), jnp.bfloat16),
            pltpu.VMEM((rows, kv), jnp.float32),
            pltpu.VMEM(mix.shape[::-1], mix.dtype),
            pltpu.SemaphoreType.DMA((n_tiles, NSH)),
            pltpu.SemaphoreType.DMA((2,)),
            pltpu.SemaphoreType.DMA,
            pltpu.SemaphoreType.DMA,
        ]
    )
    hbm = pl.BlockSpec(memory_space=pl.ANY)
    return pl.pallas_call(
        functools.partial(kernel, shapes, nrep, k_chunks),
        out_shape=pltpu.VMEM(params.shape, jnp.float32),
        in_specs=[hbm, hbm, hbm, hbm],
        out_specs=pl.BlockSpec(memory_space=pltpu.VMEM),
        scratch_shapes=scratch,
        compiler_params=pltpu.CompilerParams(
            collective_id=0, has_side_effects=True, vmem_limit_bytes=61 << 20
        ),
        name="gossip_step",
    )(params, inputs, cotangent, mix.T)


def solution(mesh):
    return jax.shard_map(
        functools.partial(on_device, mesh.shape["blk"]),
        mesh=mesh,
        in_specs=(P("blk", "fsdp", None), P("blk", "fsdp", None), P("blk", "fsdp", None), P()),
        out_specs=P("blk", "fsdp", None),
        check_vma=False,
    )
```

```python
import functools

import jax
import jax.numpy as jnp
from jax import lax
from jax.experimental import pallas as pl
from jax.experimental.pallas import tpu as pltpu
from jax.sharding import PartitionSpec as P

MIX_DENOM = 64
RATE = 0.03
LEVELS = 32767.0
TINY = 1e-30
MESH = pl.DeviceIdType.MESH

NY = 4
NX = 2
NSH = NY * NX
TILE = 128
R = 128
LA = 384

UP, DN = 0, 1
CUT = 256


def message_shapes(kv):
    h, lb = R // 2, kv - LA
    return dict(
        ax=(1, NY, R, LA),
        by1=(2, 4, h, lb),
        mid=(2, 2, h, kv),
        bx=(1, 2, h, lb),
        ay2=(2, 1, h, LA),
        u=(1, R // 16, 16, kv),
    )


def kernel(shapes, nrep, k_chunks, *refs):
    names = list(shapes)
    (params, inputs, cot_hbm, mix, out), refs = refs[:5], refs[5:]
    nm = len(names)
    sendq, sends = dict(zip(names, refs[:nm])), dict(zip(names, refs[nm : 2 * nm]))
    recvq, recvs = dict(zip(names, refs[2 * nm : 3 * nm])), dict(zip(names, refs[3 * nm : 4 * nm]))
    refs = refs[4 * nm :]
    sem_s, sem_r = dict(zip(names, refs[:nm])), dict(zip(names, refs[nm : 2 * nm]))
    part, xbuf, cot, pbuf, mbuf, sem_x, sem_c, sem_p, sem_m = refs[2 * nm :]

    tokens, kv = cot.shape
    n_tiles = xbuf.shape[0]
    sub = TILE // R
    shard_rows = TILE * n_tiles
    h = R // 2
    lb = kv - LA
    A, B = slice(0, LA), slice(LA, kv)
    H = (slice(0, h), slice(h, R))

    rep = lax.axis_index("blk")
    fs = lax.axis_index("fsdp")
    y, x = fs // NX, fs % NX
    y_up, y_dn, y_far = (y + 1) % NY, (y + NY - 1) % NY, (y + 2) % NY
    dev = dict(
        up=(rep, y_up * NX + x),
        dn=(rep, y_dn * NX + x),
        x=(rep, y * NX + (1 - x)),
        right=((rep + 1) % nrep, fs),
        left=((rep + nrep - 1) % nrep, fs),
    )

    def shard(yy, xx):
        return yy * NX + xx

    def load_x(c, f):
        return pltpu.make_async_copy(
            inputs.at[0, :, pl.ds(pl.multiple_of(f * shard_rows + c * TILE, TILE), TILE)],
            xbuf.at[c, :, pl.ds(pl.multiple_of(f * TILE, TILE), TILE)],
            sem_x.at[c, f],
        )

    early, late = slice(CUT, kv), slice(0, CUT)

    def load_cot(i, cols):
        return pltpu.make_async_copy(cot_hbm.at[0, :, cols], cot.at[:, cols], sem_c.at[i])

    load_p = pltpu.make_async_copy(params.at[0], pbuf, sem_p)
    load_mix = pltpu.make_async_copy(mix, mbuf, sem_m)
    def tile_x(yy):
        return [load_x(0, shard(yy, xx)) for xx in range(NX)]

    load_cot(0, early).start()
    for yy in (y_far, y_up):
        for load in tile_x(yy):
            load.start()
    for yy in (y_dn, y):
        for load in tile_x(yy):
            load.start()
    load_cot(1, late).start()

    barrier = pltpu.get_barrier_semaphore()
    for d in dev.values():
        pl.semaphore_signal(barrier, inc=1, device_id=d, device_id_type=MESH)

    def copies(name, d, k, to):
        return [
            pltpu.make_async_remote_copy(
                src_ref=src.at[0 if name == "u" else d, k],
                dst_ref=dst.at[d, k],
                send_sem=sem_s[name].at[d, i, k],
                recv_sem=sem_r[name].at[d, i, k],
                device_id=dev[to],
                device_id_type=MESH,
            )
            for i, (src, dst) in enumerate(
                ((sendq[name], recvq[name]), (sends[name], recvs[name]))
            )
        ]

    TO = dict(ax=("x",), bx=("x",), u=("right", "left"))

    def target(name, d):
        return TO.get(name, ("up", "dn"))[d]

    def send(name, d, k):
        for c in copies(name, d, k, target(name, d)):
            c.start()

    def arrived(name, d, k):
        for c in copies(name, d, k, target(name, d)):
            c.wait_recv()

    def sent(name, d, k):
        for c in copies(name, d, k, target(name, d)):
            c.wait_send()

    def encode(name, d, k, blocks, cols=None):
        top = functools.reduce(jnp.maximum, [jnp.abs(b()) for b in blocks])
        top = jnp.maximum(jnp.max(top, axis=0, keepdims=True), TINY)
        cols = slice(0, top.shape[1]) if cols is None else cols
        sends[name][d, k, :, cols] = top * (1.0 / LEVELS)
        inv = LEVELS / top
        for i, b in enumerate(blocks):
            sendq[name][d, k, i, :, cols] = jnp.round(b() * inv).astype(jnp.int32).astype(jnp.int16)

    def decode(name, d, k, i, cols=None):
        cols = slice(0, recvs[name].shape[-1]) if cols is None else cols
        q = recvq[name][d, k, i, :, cols].astype(jnp.int32).astype(jnp.float32)
        return q * recvs[name][d, k, :, cols]

    def at(k, f, rows, cols):
        return lambda: part[k, f, rows, cols]

    def multiply(c, j, cols=slice(0, kv)):
        lhs = xbuf[c, :, pl.ds(pl.multiple_of(j * (2 * TILE), 2 * TILE), 2 * TILE)]
        prod = lax.dot_general(
            lhs, cot[:, cols], (((0,), (0,)), ((), ())), preferred_element_type=jnp.float32
        )
        for a in range(2):
            for i in range(sub):
                lo = a * TILE + i * R
                part[c * sub + i, 2 * j + a, :, cols] = prod[lo : lo + R]

    BY1 = {UP: (y_up, H[1], H[0]), DN: (y_dn, H[0], H[1])}

    def first_y(k, d):
        near, relay, plain = BY1[d]
        encode(
            "by1",
            d,
            k,
            [at(k, shard(y_far, xx), relay, B) for xx in range(NX)]
            + [at(k, shard(near, xx), plain, B) for xx in range(NX)],
        )
        send("by1", d, k)

    def first_x(k):
        encode("ax", 0, k, [at(k, shard(yy, 1 - x), slice(0, R), A) for yy in range(NY)])
        send("ax", 0, k)

    def stage1(k):
        first_x(k)
        for d in (UP, DN):
            first_y(k, d)

    def stage2(k):
        for d in (UP, DN):
            near, relay, _ = BY1[d]
            arrived("by1", d, k)
            for xx in range(NX):
                part[k, shard(near, xx), relay, B] += decode("by1", d, k, xx)
            encode("mid", d, k, [at(k, shard(near, xx), relay, B) for xx in range(NX)], B)
        arrived("ax", 0, k)
        for yy in range(NY):
            part[k, shard(yy, x), :, A] += decode("ax", 0, k, yy)
        for d in (UP, DN):
            near, relay, plain = BY1[d]
            blocks = [at(k, shard(y_far, x), relay, A), at(k, shard(near, x), plain, A)]
            encode("mid", d, k, blocks, A)
            send("mid", d, k)

    def stage3(k):
        for d in (UP, DN):
            arrived("mid", d, k)
        for xx in (1 - x, x):
            part[k, shard(y, xx), H[0], B] += decode("by1", UP, k, 2 + xx) + decode("mid", DN, k, xx, B)
            part[k, shard(y, xx), H[1], B] += decode("by1", DN, k, 2 + xx) + decode("mid", UP, k, xx, B)
        encode("bx", 0, k, [at(k, shard(y, 1 - x), rows, B) for rows in H])
        send("bx", 0, k)
        for d in (UP, DN):
            near, relay, _ = BY1[d]
            part[k, shard(near, x), relay, A] += decode("mid", d, k, 0, A)
            encode("ay2", d, k, [at(k, shard(near, x), relay, A)])
            send("ay2", d, k)

    def stage4(k):
        for d in (UP, DN):
            arrived("ay2", d, k)
        arrived("bx", 0, k)
        mine = shard(y, x)
        base = pl.multiple_of(k * R, R)
        for half in (0, 1):
            d1, d2 = ((UP, DN), (DN, UP))[half]
            rows = H[half]
            prow = pl.ds(base + half * h, h)
            g = part[k, mine, rows, A] + decode("mid", d1, k, 1, A) + decode("ay2", d2, k, 0)
            part[k, mine, rows, A] = pbuf[prow, A] - RATE * g
            g = part[k, mine, rows, B] + decode("bx", 0, k, half)
            part[k, mine, rows, B] = pbuf[prow, B] - RATE * g
        n = R // 16
        encode("u", 0, k, [at(k, mine, slice(16 * i, 16 * i + 16), slice(0, kv)) for i in range(n)])
        for core, order in ((0, (1, 0)), (1, (0, 1))):

            @pl.when(rep % 2 == core)
            def _(order=order):
                for d in order:
                    send("u", d, k)

    def stage5(k):
        for d in (0, 1):
            arrived("u", d, k)
        mine = shard(y, x)
        column = lax.broadcasted_iota(jnp.int32, mbuf.shape, 1) == rep
        coeff = jnp.where(column, mbuf[...].astype(jnp.float32) * (1.0 / MIX_DENOM), 0.0)
        coeff = jnp.sum(coeff, axis=1, keepdims=True)
        c_left, c_self, c_right = coeff[0:1], coeff[1:2], coeff[2:3]
        for i in range(R // 16):
            rows = slice(16 * i, 16 * i + 16)
            out[0, pl.ds(pl.multiple_of(k * R + 16 * i, 16), 16)] = (
                c_left * decode("u", 0, k, i)
                + c_self * part[k, mine, rows]
                + c_right * decode("u", 1, k, i)
            )

    load_cot(0, early).wait()
    per_tile = NSH // 2

    @pl.loop(0, NY)
    def _(i):
        yy = (y + 2 - i + 3 * (i // 2) - 2 * (i // 3) + NY) % NY
        for load in tile_x(yy):
            load.wait()
        multiply(0, yy, early)

        @pl.when(i == 1)
        def _():
            pl.semaphore_wait(barrier, len(dev))
            first_y(0, UP)

        @pl.when(i == 2)
        def _():
            for c in range(1, n_tiles):
                for f in range(NSH):
                    load_x(c, f).start()
            load_p.start()
            load_mix.start()
            first_y(0, DN)

    load_cot(1, late).wait()

    @pl.loop(0, per_tile)
    def _(j):
        multiply(0, j, late)

    first_x(0)

    share = per_tile // sub

    @pl.loop(0, k_chunks + 4)
    def _(s):
        @pl.when((s >= 1) & (s < k_chunks))
        def _():
            stage1(s)

        c = s // sub + 1

        @pl.when(c < n_tiles)
        def _():
            @pl.when(s % sub == 0)
            def _():
                for f in range(NSH):
                    load_x(c, f).wait()

            @pl.loop(0, share)
            def _(j):
                multiply(c, (s % sub) * share + j)

        @pl.when(s == 0)
        def _():
            load_p.wait()
            load_mix.wait()

        for lag, stage in ((1, stage2), (2, stage3), (3, stage4), (4, stage5)):

            @pl.when((s >= lag) & (s < k_chunks + lag))
            def _(lag=lag, stage=stage):
                stage(s - lag)

    @pl.loop(0, k_chunks)
    def _(k):
        for name, shape in shapes.items():
            for d in range(2 if name == "u" else shape[0]):
                sent(name, d, k)


def on_device(nrep, params, inputs, cotangent, mix):
    _, tokens, width = inputs.shape
    kv = cotangent.shape[-1]
    rows = params.shape[1]
    n_tiles = rows // TILE
    k_chunks = rows // R
    shapes = message_shapes(kv)
    names = list(shapes)
    landing = {n: (2 if n == "u" else s[0],) + s[1:] for n, s in shapes.items()}

    def data(table):
        return [pltpu.VMEM((s[0], k_chunks) + s[1:], jnp.int16) for s in table.values()]

    def scales(table):
        return [pltpu.VMEM((s[0], k_chunks, 1, s[3]), jnp.float32) for s in table.values()]

    sems = [pltpu.SemaphoreType.DMA((landing[n][0], 2, k_chunks)) for n in names]
    scratch = (
        data(shapes)
        + scales(shapes)
        + data(landing)
        + scales(landing)
        + sems
        + sems
        + [
            pltpu.VMEM((k_chunks, NSH, R, kv), jnp.float32),
            pltpu.VMEM((n_tiles, tokens, NSH * TILE), jnp.bfloat16),
            pltpu.VMEM((tokens, kv), jnp.bfloat16),
            pltpu.VMEM((rows, kv), jnp.float32),
            pltpu.VMEM(mix.shape[::-1], mix.dtype),
            pltpu.SemaphoreType.DMA((n_tiles, NSH)),
            pltpu.SemaphoreType.DMA((2,)),
            pltpu.SemaphoreType.DMA,
            pltpu.SemaphoreType.DMA,
        ]
    )
    hbm = pl.BlockSpec(memory_space=pl.ANY)
    return pl.pallas_call(
        functools.partial(kernel, shapes, nrep, k_chunks),
        out_shape=pltpu.VMEM(params.shape, jnp.float32),
        in_specs=[hbm, hbm, hbm, hbm],
        out_specs=pl.BlockSpec(memory_space=pltpu.VMEM),
        scratch_shapes=scratch,
        compiler_params=pltpu.CompilerParams(
            collective_id=0, has_side_effects=True, vmem_limit_bytes=61 << 20
        ),
        name="gossip_step",
    )(params, inputs, cotangent, mix.T)


def solution(mesh):
    return jax.shard_map(
        functools.partial(on_device, mesh.shape["blk"]),
        mesh=mesh,
        in_specs=(P("blk", "fsdp", None), P("blk", "fsdp", None), P("blk", "fsdp", None), P()),
        out_specs=P("blk", "fsdp", None),
        check_vma=False,
    )
```

```python
import functools

import jax
import jax.numpy as jnp
from jax import lax
from jax.experimental import pallas as pl
from jax.experimental.pallas import tpu as pltpu
from jax.sharding import PartitionSpec as P

MIX_DENOM = 64
RATE = 0.03
LEVELS = 32767.0
TINY = 1e-30
MESH = pl.DeviceIdType.MESH

NY = 4
NX = 2
NSH = NY * NX
TILE = 128
R = 128
LA = 384

UP, DN = 0, 1
U = ("u0", "u1")
CUT = 256


def message_shapes(kv):
    h, lb = R // 2, kv - LA
    return dict(
        ax=(1, NY, R, LA),
        by1=(2, 4, h, lb),
        mid=(2, 2, h, kv),
        bx=(1, 2, h, lb),
        ay2=(2, 1, h, LA),
        u0=(1, h // 16, 16, kv),
        u1=(1, h // 16, 16, kv),
    )


def kernel(shapes, nrep, k_chunks, *refs):
    names = list(shapes)
    (params, inputs, cot_hbm, mix, out), refs = refs[:5], refs[5:]
    nm = len(names)
    sendq, sends = dict(zip(names, refs[:nm])), dict(zip(names, refs[nm : 2 * nm]))
    recvq, recvs = dict(zip(names, refs[2 * nm : 3 * nm])), dict(zip(names, refs[3 * nm : 4 * nm]))
    refs = refs[4 * nm :]
    sem_s, sem_r = dict(zip(names, refs[:nm])), dict(zip(names, refs[nm : 2 * nm]))
    part, xbuf, cot, pbuf, mbuf, sem_x, sem_c, sem_p, sem_m = refs[2 * nm :]

    tokens, kv = cot.shape
    n_tiles = xbuf.shape[0]
    sub = TILE // R
    shard_rows = TILE * n_tiles
    h = R // 2
    lb = kv - LA
    A, B = slice(0, LA), slice(LA, kv)
    H = (slice(0, h), slice(h, R))

    rep = lax.axis_index("blk")
    fs = lax.axis_index("fsdp")
    y, x = fs // NX, fs % NX
    y_up, y_dn, y_far = (y + 1) % NY, (y + NY - 1) % NY, (y + 2) % NY
    dev = dict(
        up=(rep, y_up * NX + x),
        dn=(rep, y_dn * NX + x),
        x=(rep, y * NX + (1 - x)),
        right=((rep + 1) % nrep, fs),
        left=((rep + nrep - 1) % nrep, fs),
    )

    def shard(yy, xx):
        return yy * NX + xx

    def load_x(c, f):
        return pltpu.make_async_copy(
            inputs.at[0, :, pl.ds(pl.multiple_of(f * shard_rows + c * TILE, TILE), TILE)],
            xbuf.at[c, :, pl.ds(pl.multiple_of(f * TILE, TILE), TILE)],
            sem_x.at[c, f],
        )

    early, late = slice(CUT, kv), slice(0, CUT)

    def load_cot(i, cols):
        return pltpu.make_async_copy(cot_hbm.at[0, :, cols], cot.at[:, cols], sem_c.at[i])

    load_p = pltpu.make_async_copy(params.at[0], pbuf, sem_p)
    load_mix = pltpu.make_async_copy(mix, mbuf, sem_m)
    def tile_x(yy):
        return [load_x(0, shard(yy, xx)) for xx in range(NX)]

    load_cot(0, early).start()
    for yy in (y_far, y_up):
        for load in tile_x(yy):
            load.start()
    for yy in (y_dn, y):
        for load in tile_x(yy):
            load.start()
    load_cot(1, late).start()

    barrier = pltpu.get_barrier_semaphore()
    for d in dev.values():
        pl.semaphore_signal(barrier, inc=1, device_id=d, device_id_type=MESH)

    def copies(name, d, k, to):
        return [
            pltpu.make_async_remote_copy(
                src_ref=src.at[0 if name in U else d, k],
                dst_ref=dst.at[d, k],
                send_sem=sem_s[name].at[d, i, k],
                recv_sem=sem_r[name].at[d, i, k],
                device_id=dev[to],
                device_id_type=MESH,
            )
            for i, (src, dst) in enumerate(
                ((sendq[name], recvq[name]), (sends[name], recvs[name]))
            )
        ]

    TO = dict(ax=("x",), bx=("x",), u0=("right", "left"), u1=("right", "left"))

    def target(name, d):
        return TO.get(name, ("up", "dn"))[d]

    def send(name, d, k):
        for c in copies(name, d, k, target(name, d)):
            c.start()

    def arrived(name, d, k):
        for c in copies(name, d, k, target(name, d)):
            c.wait_recv()

    def sent(name, d, k):
        for c in copies(name, d, k, target(name, d)):
            c.wait_send()

    def encode(name, d, k, blocks, cols=None):
        top = functools.reduce(jnp.maximum, [jnp.abs(b()) for b in blocks])
        top = jnp.maximum(jnp.max(top, axis=0, keepdims=True), TINY)
        cols = slice(0, top.shape[1]) if cols is None else cols
        sends[name][d, k, :, cols] = top * (1.0 / LEVELS)
        inv = LEVELS / top
        for i, b in enumerate(blocks):
            sendq[name][d, k, i, :, cols] = jnp.round(b() * inv).astype(jnp.int32).astype(jnp.int16)

    def decode(name, d, k, i, cols=None):
        cols = slice(0, recvs[name].shape[-1]) if cols is None else cols
        q = recvq[name][d, k, i, :, cols].astype(jnp.int32).astype(jnp.float32)
        return q * recvs[name][d, k, :, cols]

    def at(k, f, rows, cols):
        return lambda: part[k, f, rows, cols]

    def multiply(c, j, cols=slice(0, kv)):
        lhs = xbuf[c, :, pl.ds(pl.multiple_of(j * (2 * TILE), 2 * TILE), 2 * TILE)]
        prod = lax.dot_general(
            lhs, cot[:, cols], (((0,), (0,)), ((), ())), preferred_element_type=jnp.float32
        )
        for a in range(2):
            for i in range(sub):
                lo = a * TILE + i * R
                part[c * sub + i, 2 * j + a, :, cols] = prod[lo : lo + R]

    BY1 = {UP: (y_up, H[1], H[0]), DN: (y_dn, H[0], H[1])}

    def first_y(k, d):
        near, relay, plain = BY1[d]
        encode(
            "by1",
            d,
            k,
            [at(k, shard(y_far, xx), relay, B) for xx in range(NX)]
            + [at(k, shard(near, xx), plain, B) for xx in range(NX)],
        )
        send("by1", d, k)

    def first_x(k):
        encode("ax", 0, k, [at(k, shard(yy, 1 - x), slice(0, R), A) for yy in range(NY)])
        send("ax", 0, k)

    def stage1(k):
        first_x(k)
        for d in (UP, DN):
            first_y(k, d)

    def stage2(k):
        def add_x(yy):
            part[k, shard(yy, x), :, A] += decode("ax", 0, k, yy)

        for d in (UP, DN):
            near, relay, plain = BY1[d]
            arrived("by1", d, k)
            for xx in range(NX):
                part[k, shard(near, xx), relay, B] += decode("by1", d, k, xx)
            encode("mid", d, k, [at(k, shard(near, xx), relay, B) for xx in range(NX)], B)
            if d == UP:
                arrived("ax", 0, k)
                add_x(y_far)
            add_x(near)
            blocks = [at(k, shard(y_far, x), relay, A), at(k, shard(near, x), plain, A)]
            encode("mid", d, k, blocks, A)
            send("mid", d, k)
        add_x(y)

    def stage3(k):
        def add_y(xx):
            for up, rows in ((0, H[1]), (1, H[0])):
                one, two = ((DN, UP), (UP, DN))[up]
                part[k, shard(y, xx), rows, B] += decode("by1", one, k, 2 + xx) + decode(
                    "mid", two, k, xx, B
                )

        for d in (UP, DN):
            arrived("mid", d, k)
        add_y(1 - x)
        encode("bx", 0, k, [at(k, shard(y, 1 - x), rows, B) for rows in H])
        send("bx", 0, k)
        for d in (UP, DN):
            near, relay, _ = BY1[d]
            part[k, shard(near, x), relay, A] += decode("mid", d, k, 0, A)
            encode("ay2", d, k, [at(k, shard(near, x), relay, A)])
            send("ay2", d, k)
        add_y(x)

    def stage4(k):
        arrived("bx", 0, k)
        mine = shard(y, x)
        base = pl.multiple_of(k * R, R)
        for half, name in enumerate(U):
            d1, d2 = ((UP, DN), (DN, UP))[half]
            arrived("ay2", d2, k)
            rows = H[half]
            prow = pl.ds(base + half * h, h)
            g = part[k, mine, rows, A] + decode("mid", d1, k, 1, A) + decode("ay2", d2, k, 0)
            part[k, mine, rows, A] = pbuf[prow, A] - RATE * g
            g = part[k, mine, rows, B] + decode("bx", 0, k, half)
            part[k, mine, rows, B] = pbuf[prow, B] - RATE * g
            starts = [half * h + 16 * i for i in range(h // 16)]
            encode(name, 0, k, [at(k, mine, slice(i, i + 16), slice(0, kv)) for i in starts])
            for d in (0, 1):
                send(name, d, k)

    def stage5(k):
        mine = shard(y, x)
        column = lax.broadcasted_iota(jnp.int32, mbuf.shape, 1) == rep
        coeff = jnp.where(column, mbuf[...].astype(jnp.float32) * (1.0 / MIX_DENOM), 0.0)
        coeff = jnp.sum(coeff, axis=1, keepdims=True)
        c_left, c_self, c_right = coeff[0:1], coeff[1:2], coeff[2:3]
        for half, name in enumerate(U):
            for d in (0, 1):
                arrived(name, d, k)
            for i in range(h // 16):
                row = half * h + 16 * i
                out[0, pl.ds(pl.multiple_of(k * R + row, 16), 16)] = (
                    c_left * decode(name, 0, k, i)
                    + c_self * part[k, mine, row : row + 16]
                    + c_right * decode(name, 1, k, i)
                )

    load_cot(0, early).wait()
    per_tile = NSH // 2

    @pl.loop(0, NY)
    def _(i):
        yy = (y + 2 - i + 3 * (i // 2) - 2 * (i // 3) + NY) % NY
        for load in tile_x(yy):
            load.wait()
        multiply(0, yy, early)

        @pl.when(i == 1)
        def _():
            pl.semaphore_wait(barrier, len(dev))
            first_y(0, UP)

        @pl.when(i == 2)
        def _():
            for c in range(1, n_tiles):
                for f in range(NSH):
                    load_x(c, f).start()
            load_p.start()
            load_mix.start()
            first_y(0, DN)

    load_cot(1, late).wait()

    @pl.loop(0, per_tile)
    def _(j):
        multiply(0, j, late)

    first_x(0)

    share = per_tile // sub

    @pl.loop(0, k_chunks + 4)
    def _(s):
        @pl.when((s >= 1) & (s < k_chunks))
        def _():
            stage1(s)

        c = s // sub + 1

        @pl.when(c < n_tiles)
        def _():
            @pl.when(s % sub == 0)
            def _():
                for f in range(NSH):
                    load_x(c, f).wait()

            @pl.loop(0, share)
            def _(j):
                multiply(c, (s % sub) * share + j)

        @pl.when(s == 0)
        def _():
            load_p.wait()
            load_mix.wait()

        for lag, stage in ((1, stage2), (2, stage3), (3, stage4), (4, stage5)):

            @pl.when((s >= lag) & (s < k_chunks + lag))
            def _(lag=lag, stage=stage):
                stage(s - lag)

    @pl.loop(0, k_chunks)
    def _(k):
        for name, shape in shapes.items():
            for d in range(2 if name in U else shape[0]):
                sent(name, d, k)


def on_device(nrep, params, inputs, cotangent, mix):
    _, tokens, width = inputs.shape
    kv = cotangent.shape[-1]
    rows = params.shape[1]
    n_tiles = rows // TILE
    k_chunks = rows // R
    shapes = message_shapes(kv)
    names = list(shapes)
    landing = {n: (2 if n in U else s[0],) + s[1:] for n, s in shapes.items()}

    def data(table):
        return [pltpu.VMEM((s[0], k_chunks) + s[1:], jnp.int16) for s in table.values()]

    def scales(table):
        return [pltpu.VMEM((s[0], k_chunks, 1, s[3]), jnp.float32) for s in table.values()]

    sems = [pltpu.SemaphoreType.DMA((landing[n][0], 2, k_chunks)) for n in names]
    scratch = (
        data(shapes)
        + scales(shapes)
        + data(landing)
        + scales(landing)
        + sems
        + sems
        + [
            pltpu.VMEM((k_chunks, NSH, R, kv), jnp.float32),
            pltpu.VMEM((n_tiles, tokens, NSH * TILE), jnp.bfloat16),
            pltpu.VMEM((tokens, kv), jnp.bfloat16),
            pltpu.VMEM((rows, kv), jnp.float32),
            pltpu.VMEM(mix.shape[::-1], mix.dtype),
            pltpu.SemaphoreType.DMA((n_tiles, NSH)),
            pltpu.SemaphoreType.DMA((2,)),
            pltpu.SemaphoreType.DMA,
            pltpu.SemaphoreType.DMA,
        ]
    )
    hbm = pl.BlockSpec(memory_space=pl.ANY)
    return pl.pallas_call(
        functools.partial(kernel, shapes, nrep, k_chunks),
        out_shape=pltpu.VMEM(params.shape, jnp.float32),
        in_specs=[hbm, hbm, hbm, hbm],
        out_specs=pl.BlockSpec(memory_space=pltpu.VMEM),
        scratch_shapes=scratch,
        compiler_params=pltpu.CompilerParams(
            collective_id=0, has_side_effects=True, vmem_limit_bytes=61 << 20
        ),
        name="gossip_step",
    )(params, inputs, cotangent, mix.T)


def solution(mesh):
    return jax.shard_map(
        functools.partial(on_device, mesh.shape["blk"]),
        mesh=mesh,
        in_specs=(P("blk", "fsdp", None), P("blk", "fsdp", None), P("blk", "fsdp", None), P()),
        out_specs=P("blk", "fsdp", None),
        check_vma=False,
    )
```
